32 devices in a mesh: lat: 16 (over z, y, core), fld: 2 (over x).
Axes of the slice: x: 2, y: 2, z: 4, core: 2. Of those that a mesh axis runs over, the one named last changes fastest.
Arguments:
- spectra: bfloat16 [2, 1280, 16, 1280], P(None, 'lat', 'fld'), may hold values from -0.19921875 to 0.19921875
- legendre: bfloat16 [1280, 16, 1280], P('lat'), may hold values from -0.15625 to 0.15625
- wave_order: int32 [1280], replicated, may hold values from 0 to 1279, each once
- row_points: int32 [16], replicated, may hold values from 1300 to 5136, as said below
- owners: int32 [1312, 1], replicated, may hold values from 0 to 15; in each aligned block of 82 rows (0 to 81, 82 to 163, ...) at most 6 rows name the same one
Outputs:
- cell_slots: bfloat16 [1536, 16, 128], P(('lat', 'fld'))
The draws below stay inside these ranges and needn't reach their ends.
Inputs may be any that keep to these rules, and one draw needn't show every extreme that they name: `row_points`: the values are 20 + 4 k for distinct whole k, increasing along the pairs; the last pair has 5136 points. `owners`: within the 82 blocks of one row pair (rows p * 82 to p * 82 + 81) no owner is named more than 6 times; some owner is named exactly 6 times in some pairs. `wave_order`: each wavenumber stands in exactly one slot.
All inputs are finite; a program needn't handle non-finite values.
Results may differ from the reference program's by a relative error of at most 0.0055.
Values may be sent and summed in bfloat16 or wider, within the bound.
A program may use at most 64 MiB of HBM per device.

```python
import math
import jax
import jax.numpy as jnp
import numpy as np
from jax import lax

M = 1280
CELL = 128
CH = 16
LATP = 16
BPR = 41
GB = 82
SEND = 6
N_LAT = 16


def draw_row_points(key, part):
    span_count = M - 1 - M // 4
    picked = jax.random.permutation(key, span_count)[:LATP - 1] + M // 4
    latitude_rows = jnp.sort(jnp.concatenate([picked.astype(jnp.int32), jnp.full((1,), M - 1, jnp.int32)]))
    return (20 + 4 * latitude_rows).astype(jnp.int32)


def level_of(key, extent, pieces, low, high):
    gain = 1.0
    for position, blocks in pieces:
        steps = jax.random.uniform(jax.random.fold_in(jax.random.fold_in(key, 6), position), (blocks,), jnp.float32, low / len(pieces), high / len(pieces))
        gain = gain * jnp.repeat(jnp.exp(steps), extent[position] // blocks).reshape((-1,) + (1,) * (len(extent) - 1 - position))
    return gain


def deal_out(rng, own, number, rows, count, top, reach, lean):
    sequence = jax.random.permutation(rng, count)
    packed, common = portions_of(count, rows * top, reach, lean, True), portions_of(count, rows * top, reach, lean, False)
    places = jnp.arange(count)

    def named(tallies, turn):
        used = int((tallies > 0).sum())
        fixed = max(1, used // 4)
        shifted = fixed + (places - fixed + turn * (used - fixed)) % max(1, count - fixed)
        return jnp.zeros((count,), jnp.int32).at[sequence[jnp.where(places < fixed, places, shifted)]].set(jnp.asarray(tallies, jnp.int32))

    tallies = jnp.where(number % 4 == 0, named(packed, number // 4), named(common, number - number // 4 - 1))
    mixed = jax.random.permutation(jax.random.fold_in(own, 3), count)
    giver, sink = mixed[0:count // 2 * 2:2], mixed[1:count // 2 * 2:2]
    slack = jnp.minimum(tallies[giver] - 1, reach - tallies[sink]) // 2
    slack = jnp.where((giver == sequence[0]) | (sink == sequence[0]) | (tallies[sink] == 0), 0, jnp.maximum(slack, 0))
    shifted = jax.random.randint(jax.random.fold_in(own, 4), (count // 2,), 0, 1 << 20) % (slack + 1)
    tallies = tallies.at[giver].add(-shifted).at[sink].add(shifted)
    labels = jnp.searchsorted(jnp.cumsum(tallies), jnp.arange(rows * top), side="right").astype(jnp.int32)
    grid = labels.reshape(top, rows).T
    grid = grid[jax.random.permutation(jax.random.fold_in(own, 1), rows)]
    turn = jax.random.randint(jax.random.fold_in(own, 2), (rows, 1), 0, top)
    return jnp.take_along_axis(grid, (jnp.arange(top)[None, :] + turn) % top, axis=1)


def portions_of(number_of, total, bound, lean, full):
    loads = [(1 << 20) // math.isqrt(grade ** lean) + 1 for grade in range(1, number_of + 1)]
    largest = bound if full else min(bound, max(-(-total // number_of), total * loads[0] // sum(loads)))
    least = 1 if total - largest >= number_of - 1 else 0
    given, rest = [largest] + [least] * (number_of - 1), total - largest - least * (number_of - 1)
    while rest > 0:
        candidates = [i for i in range(1, number_of) if given[i] < largest] or [i for i in range(1, number_of) if given[i] < bound]
        mass, left = sum([loads[i] for i in candidates]), rest
        for i in candidates:
            extra = min(bound - given[i], max(1, left * loads[i] // mass), rest)
            given[i] = given[i] + extra
            rest = rest - extra
    return np.array(given)


def noise(key, dims, scale, most, cuts=(), held_as=jnp.bfloat16):
    array = jax.random.normal(key, dims, jnp.float32) * scale
    if len(cuts) > 0:
        array = level_of(key, dims, cuts, -0.22, 0.18) * array
    return jnp.clip(array, min=-most, max=most).astype(held_as)


def setup_inputs(seed: int = 0) -> dict:
    key_of = jax.random.split(jax.random.key(seed), 6)
    spectra = noise(key_of[0], (2, M, CH, M), 0.03, 0.19921875, ((1, 16), (2, 2)))
    legendre = noise(key_of[1], (M, LATP, M), M ** -0.5, 0.15625, ((0, 16),))
    wave_order = jax.random.permutation(key_of[2], M).astype(jnp.int32)
    row_points = draw_row_points(jax.random.fold_in(key_of[5], 71), 0)
    owners_keys = jax.random.split(jax.random.fold_in(key_of[4], 1), (LATP * GB) // GB)
    owners_turns = jax.random.permutation(jax.random.fold_in(key_of[4], 3), (LATP * GB) // GB)
    owners = jax.vmap(lambda own, number: deal_out(jax.random.fold_in(key_of[4], 2), own, number, GB, N_LAT, 1, SEND, 1))(owners_keys, owners_turns).reshape((LATP * GB, 1))
    return {"spectra": spectra, "legendre": legendre, "wave_order": wave_order, "row_points": row_points, "owners": owners}


TWO_PI = 6.283185307179586


def make_basis(wave_list, points_row, first_point, span_width):
    columns = first_point + lax.iota(jnp.int32, span_width)
    remain = (wave_list[:, None] * columns[None, :]) % points_row
    angles = remain.astype(jnp.float32) * TWO_PI / points_row.astype(jnp.float32)
    weights = jnp.where(wave_list == 0, 1.0, 2.0).astype(jnp.float32)[:, None]
    return jnp.concatenate([weights * jnp.cos(angles), -(weights * jnp.sin(angles))], 0).astype(jnp.bfloat16)


def synthesize(left_rows, wave_list, points_row, first_point, span_width):
    basis_rows = make_basis(wave_list, points_row, first_point, span_width)
    values = jnp.dot(left_rows, basis_rows, preferred_element_type=jnp.float32)
    inside = (first_point + lax.iota(jnp.int32, span_width)) < points_row
    return jnp.where(inside[None, :], values, jnp.zeros((), jnp.float32)).astype(jnp.bfloat16)


def reference(spectra, legendre, wave_order, row_points, owners):
    degrees = lax.iota(jnp.int32, M)
    parity_sign = jnp.where(degrees % 2 == 0, 1.0, -1.0).astype(jnp.float32)

    def one_slot(slot_items):
        coefficient, legendre_slot, wave_number = slot_items
        kept_mask = degrees < M - wave_number
        values = jnp.where(kept_mask[None, None, :], coefficient.astype(jnp.float32), jnp.zeros((), jnp.float32))
        table_wide = legendre_slot.astype(jnp.float32)
        north_sum = jnp.einsum("ick,pk->pci", values, table_wide)
        south_sum = jnp.einsum("ick,pk->pci", values * parity_sign, table_wide)
        return jnp.stack([north_sum, south_sum], 1).astype(jnp.bfloat16)

    fourier = lax.map(one_slot, (jnp.transpose(spectra, (1, 0, 2, 3)), legendre, wave_order))

    def one_pair(pair_items):
        pair_rows, points_row = pair_items
        left_rows = jnp.transpose(pair_rows, (1, 2, 3, 0)).reshape(2 * CH, 2 * M)
        grid_rows = synthesize(left_rows, wave_order, points_row, 0, BPR * CELL)
        trimmed = grid_rows.reshape(2, CH, BPR, CELL)
        return jnp.transpose(trimmed, (0, 2, 1, 3)).reshape(2 * BPR, CH, CELL)

    blocks = lax.map(one_pair, (jnp.transpose(fourier, (1, 0, 2, 3, 4)), row_points))
    owner_grid = owners[:, 0].reshape(LATP, 2 * BPR)
    targets = lax.iota(jnp.int32, N_LAT)
    onehot = (owner_grid[:, :, None] == targets[None, None, :]).astype(jnp.int32)
    earlier = jnp.cumsum(onehot, 1) - onehot
    rank_list = jnp.sum(earlier * onehot, 2)
    target_slot = owner_grid * (LATP * SEND) + lax.iota(jnp.int32, LATP)[:, None] * SEND + rank_list
    cell_slots = jnp.zeros((N_LAT * LATP * SEND, CH, CELL), jnp.bfloat16)
    return cell_slots.at[target_slot.reshape(-1)].set(blocks.reshape(LATP * 2 * BPR, CH, CELL))
```

```python
import functools
import math

import jax
import jax.numpy as jnp
from jax import lax
from jax.experimental import pallas as pl
from jax.experimental.pallas import tpu as pltpu
from jax.sharding import PartitionSpec as P

CELL = 128
BPR = 41
LANES = 128
WIDTH = 256
STEP = 16
MESH = pl.DeviceIdType.MESH
F32 = jnp.float32
BF16 = jnp.bfloat16
I32 = jnp.int32


def nt_dot(left, right):
    return lax.dot_general(left, right, (((1,), (1,)), ((), ())), preferred_element_type=F32)


def turn_tables(wave_row, index_column, points):
    product = wave_row * index_column
    remain = product - jnp.floor(product / points) * points
    remain = jnp.where(remain < 0, remain + points, remain)
    remain = jnp.where(remain >= points, remain - points, remain)
    quarter = jnp.floor(4.0 * remain / points + 0.5)
    angle = (4.0 * remain - quarter * points) * (math.pi / 2) / points
    square = angle * angle
    sine = angle * (
        1.0
        + square
        * (
            -1.0 / 6
            + square * (1.0 / 120 + square * (-1.0 / 5040 + square * (1.0 / 362880)))
        )
    )
    cosine = 1.0 + square * (
        -0.5
        + square
        * (
            1.0 / 24
            + square * (-1.0 / 720 + square * (1.0 / 40320 - square * (1.0 / 3628800)))
        )
    )
    swap = (quarter == 1.0) | (quarter == 3.0)
    cos_turned = jnp.where(swap, sine, cosine)
    sin_turned = jnp.where(swap, cosine, sine)
    cos_turned = jnp.where((quarter == 1.0) | (quarter == 2.0), -cos_turned, cos_turned)
    sin_turned = jnp.where((quarter == 2.0) | (quarter == 3.0), -sin_turned, sin_turned)
    return cos_turned, sin_turned


def fused_kernel(
    dims,
    waves_smem,
    points_smem,
    spectra_hbm,
    legendre_hbm,
    waves_ref,
    owners_ref,
    out_ref,
    spectra_buf,
    legendre_buf,
    permuted_buf,
    first_send,
    first_recv,
    basis_buf,
    turn_cos,
    turn_sin,
    rotated_buf,
    total_buf,
    grid_buf,
    select_buf,
    second_send,
    load_sems,
    send_sems1,
    recv_sems1,
    send_sems2,
    recv_sems2,
    local_sem,
):
    (lat, fld, pairs, slots, channels, degrees, group, send_cap, blocks) = dims
    groups = slots // group
    segments = LANES // group
    rows_s = group * channels
    rows_l = group * pairs
    half_rows = blocks * 2 * channels
    padded_rows = grid_buf.shape[0] // 2
    per_fld = pairs // fld
    slot_rows = send_cap * channels
    me = lax.axis_index("lat")
    my_fld = lax.axis_index("fld")

    barrier = pltpu.get_barrier_semaphore()
    everyone = lat * fld
    my_flat = me * fld + my_fld

    def greet(step, carry):
        other = lax.rem(my_flat + step, everyone)
        pl.semaphore_signal(
            barrier, inc=1, device_id=(other // fld, lax.rem(other, fld)), device_id_type=MESH
        )
        return carry

    def loads(index):
        row_s = pl.multiple_of(index * rows_s, rows_s)
        row_l = pl.multiple_of(index * rows_l, rows_l)
        return (
            pltpu.make_async_copy(
                spectra_hbm.at[:, pl.ds(row_s, rows_s), :],
                spectra_buf.at[:, pl.ds(row_s, rows_s), :],
                load_sems.at[0, index],
            ),
            pltpu.make_async_copy(
                legendre_hbm.at[pl.ds(row_l, rows_l), :],
                legendre_buf.at[pl.ds(row_l, rows_l), :],
                load_sems.at[1, index],
            ),
        )

    for index in range(groups):
        for copy in loads(index):
            copy.start()
    lax.fori_loop(1, everyone, greet, 0)

    points = jnp.full((1, LANES), points_smem[me], I32).astype(F32)

    table_rows = turn_cos.shape[1] + 2 * STEP
    row_index = lax.broadcasted_iota(I32, (table_rows, LANES), 0)
    index_column = jnp.where(
        row_index < STEP,
        row_index,
        jnp.where(row_index < 2 * STEP, (row_index - STEP) * STEP, (row_index - 2 * STEP) * WIDTH),
    ).astype(F32)

    def make_tables(source, carry):
        wave_row = waves_ref[pl.ds(source, 1), :]
        cos_all, sin_all = turn_tables(wave_row.astype(F32), index_column, points)
        weight = jnp.where(wave_row == 0, 1.0, 2.0).astype(F32)
        turn_cos[source] = cos_all[2 * STEP :] * weight
        turn_sin[source] = sin_all[2 * STEP :] * weight
        cos_low, sin_low = cos_all[:STEP], sin_all[:STEP]
        for high in range(WIDTH // STEP):
            cos_high = cos_all[STEP + high : STEP + high + 1]
            sin_high = sin_all[STEP + high : STEP + high + 1]
            place = slice(high * STEP, (high + 1) * STEP)
            basis_buf[source, place, :LANES] = (cos_high * cos_low - sin_high * sin_low).astype(BF16)
            basis_buf[source, place, LANES:] = (sin_high * cos_low + cos_high * sin_low).astype(BF16)
        return carry

    lax.fori_loop(0, lat, make_tables, 0)

    owner_row = owners_ref[pl.ds(me, 1), :]
    onehot = (lax.broadcasted_iota(I32, (lat, LANES), 0) == owner_row).astype(F32)
    upper = (
        lax.broadcasted_iota(I32, (LANES, LANES), 0) < lax.broadcasted_iota(I32, (LANES, LANES), 1)
    ).astype(F32)
    earlier = jnp.dot(onehot.astype(BF16), upper.astype(BF16), preferred_element_type=F32)
    rank_row = jnp.sum(onehot * earlier, axis=0, keepdims=True)
    which = lax.broadcasted_iota(I32, (16, LANES), 0)
    both = jnp.where(which == 0, owner_row.astype(F32), jnp.where(which == 1, rank_row, 0.0))
    total_columns = 2 * padded_rows
    column = lax.broadcasted_iota(I32, (LANES, total_columns), 1)
    half = column // padded_rows
    inner = column - half * padded_rows
    span = inner // (2 * channels)
    mirror = (inner // channels) % 2
    block = 2 * span + half
    valid = (inner < half_rows) & (block < BPR)
    number = jnp.where(valid, mirror * BPR + block, -1)
    expand = (lax.broadcasted_iota(I32, (LANES, total_columns), 0) == number).astype(F32)
    spread = jnp.dot(both.astype(BF16), expand.astype(BF16), preferred_element_type=F32)
    spread = spread.astype(I32)
    channel = column[:1] % channels
    target = spread[0:1] * slot_rows + spread[1:2] * channels + channel
    target = jnp.where(valid[:1], target, -1)

    def make_select(index, carry):
        start = pl.multiple_of(index * LANES, LANES)
        rows = lax.broadcasted_iota(I32, (LANES, total_columns), 0) + start
        select_buf[pl.ds(start, LANES), :] = (rows == target).astype(F32).astype(BF16)
        return carry

    lax.fori_loop(0, select_buf.shape[0] // LANES, make_select, 0)

    degree = lax.broadcasted_iota(I32, (pairs, degrees), 1)
    alternate = (1 - 2 * (degree % 2)).astype(F32).astype(BF16)
    lane = lax.broadcasted_iota(I32, (channels, rows_l), 1)
    out_lane = lax.broadcasted_iota(I32, (rows_l, rows_l), 1)
    in_row = lax.broadcasted_iota(I32, (rows_l, rows_l), 0)

    def legendre_group(index, carry):
        for copy in loads(index):
            copy.wait()
        row_s = pl.multiple_of(index * rows_s, rows_s)
        row_l = pl.multiple_of(index * rows_l, rows_l)
        north_rows = []
        south_rows = []
        for slot in range(group):
            limit = degrees - waves_smem[me * slots + index * group + slot]
            keep = jnp.where(degree < limit, 1.0, 0.0).astype(F32).astype(BF16)
            table = legendre_buf[pl.ds(pl.multiple_of(row_l + slot * pairs, pairs), pairs), :] * keep
            north_rows.append(table)
            south_rows.append(table * alternate)
        values = jnp.concatenate(
            [spectra_buf[0, pl.ds(row_s, rows_s), :], spectra_buf[1, pl.ds(row_s, rows_s), :]], 0
        )
        summed = []
        for part in range(2):
            rows = north_rows if part == 0 else south_rows
            products = nt_dot(values, jnp.concatenate(rows, 0)).reshape(2, group, channels, rows_l)
            picked = []
            for part_of in range(2):
                kept = jnp.zeros((channels, rows_l), F32)
                for slot in range(group):
                    kept = jnp.where(lane // pairs == slot, products[part_of, slot], kept)
                picked.append(kept)
            summed.append(picked)
        stacked = jnp.concatenate([summed[0][0], summed[1][0], summed[0][1], summed[1][1]], 0)
        dest_half = out_lane // LANES
        segment = (out_lane % LANES) // group
        dest = dest_half * segments + lax.rem(segment - index + segments, segments)
        permute = (in_row == (out_lane % group) * pairs + dest).astype(F32).astype(BF16)
        permuted_buf[index] = jnp.dot(stacked.astype(BF16), permute, preferred_element_type=F32)
        return carry

    lax.fori_loop(0, groups, legendre_group, 0)

    lane_segment = lax.broadcasted_iota(I32, (4 * channels, LANES), 1) // group
    for pair in range(pairs):
        at = (pair // segments) * LANES
        gathered = jnp.zeros((4 * channels, LANES), F32)
        for index in range(groups):
            gathered = jnp.where(
                lane_segment == (pair % segments + index) % segments,
                permuted_buf[index, :, at : at + LANES],
                gathered,
            )
        first_send[pair] = gathered.astype(BF16)

    pl.semaphore_wait(barrier, everyone - 1)

    def first_copy(step):
        other = lax.rem(me + step, lat)
        return pltpu.make_async_remote_copy(
            src_ref=first_send.at[other],
            dst_ref=first_recv.at[me],
            send_sem=send_sems1.at[step],
            recv_sem=recv_sems1.at[step],
            device_id=(other, my_fld),
            device_id_type=MESH,
        )

    def first_start(step, carry):
        first_copy(step).start()
        return carry

    lax.fori_loop(1, lat, first_start, 0)

    def accumulate(source, arrived, first):
        real = arrived[: 2 * channels].astype(F32)
        imag = arrived[2 * channels :].astype(F32)
        cos_rows = turn_cos[source]
        sin_rows = turn_sin[source]
        for span_index in range(blocks):
            cos_turn = cos_rows[span_index : span_index + 1]
            sin_turn = sin_rows[span_index : span_index + 1]
            place = slice(span_index * 2 * channels, (span_index + 1) * 2 * channels)
            rotated_buf[place, :LANES] = (real * cos_turn - imag * sin_turn).astype(BF16)
            rotated_buf[place, LANES:] = (-(real * sin_turn + imag * cos_turn)).astype(BF16)
        product = nt_dot(rotated_buf[...], basis_buf[source])
        if first:
            total_buf[...] = product
        else:
            total_buf[...] += product

    accumulate(me, first_send[me], True)

    def arrive(step, carry):
        source = lax.rem(me + lat - step, lat)
        first_copy(step).wait_recv()
        accumulate(source, first_recv[source], False)
        return carry

    lax.fori_loop(1, lat, arrive, 0)

    point = lax.broadcasted_iota(I32, (half_rows, WIDTH), 0) // (2 * channels) * WIDTH + (
        lax.broadcasted_iota(I32, (half_rows, WIDTH), 1)
    )
    grid = jnp.where(point < points_smem[me], total_buf[...], 0.0).astype(BF16)
    grid_buf[...] = jnp.zeros(grid_buf.shape, BF16)
    grid_buf[:half_rows, :] = grid[:, :CELL]
    grid_buf[padded_rows : padded_rows + half_rows, :] = grid[:, CELL:]
    routed = jnp.dot(select_buf[...], grid_buf[...], preferred_element_type=F32).astype(BF16)
    second_send[...] = routed[: lat * slot_rows]

    home = me // per_fld
    mine = lax.rem(me, per_fld)

    def second_copy(step):
        other = lax.rem(me + step, lat)
        return pltpu.make_async_remote_copy(
            src_ref=second_send.at[pl.ds(pl.multiple_of(other * slot_rows, slot_rows), slot_rows), :],
            dst_ref=out_ref.at[my_fld, mine],
            send_sem=send_sems2.at[step],
            recv_sem=recv_sems2.at[my_fld, mine],
            device_id=(other, home),
            device_id_type=MESH,
        )

    own_copy = pltpu.make_async_copy(
        second_send.at[pl.ds(pl.multiple_of(me * slot_rows, slot_rows), slot_rows), :],
        out_ref.at[my_fld, mine],
        local_sem,
    )

    def second_start(step, carry):
        second_copy(step).start()
        return carry

    lax.fori_loop(1, lat, second_start, 0)

    @pl.when(home == my_fld)
    def _():
        own_copy.start()

    @pl.when(home != my_fld)
    def _():
        second_copy(0).start()

    def first_done(step, carry):
        first_copy(step).wait_send()
        return carry

    lax.fori_loop(1, lat, first_done, 0)

    def second_done(step, carry):
        second_copy(step).wait_send()
        return carry

    lax.fori_loop(1, lat, second_done, 0)

    @pl.when(home == my_fld)
    def _():
        own_copy.wait()

    @pl.when(home != my_fld)
    def _():
        second_copy(0).wait_send()

    def from_source(step, carry):
        from_fld = step // per_fld
        from_pair = lax.rem(step, per_fld)
        is_self = (from_fld == my_fld) & (my_fld * per_fld + from_pair == me)

        @pl.when(jnp.logical_not(is_self))
        def _():
            pltpu.make_async_remote_copy(
                src_ref=second_send.at[pl.ds(0, slot_rows), :],
                dst_ref=out_ref.at[from_fld, from_pair],
                send_sem=send_sems2.at[0],
                recv_sem=recv_sems2.at[from_fld, from_pair],
                device_id=(me, my_fld),
                device_id_type=MESH,
            ).wait_recv()

        return carry

    lax.fori_loop(0, fld * per_fld, from_source, 0)


def on_device(lat, fld, spectra, legendre, wave_order, row_points, owners):
    position = lax.axis_index("lat")
    slots, pairs, degrees = legendre.shape
    channels = spectra.shape[2]
    group = max(g for g in range(1, slots + 1) if slots % g == 0 and g * pairs <= 256 and LANES % g == 0)
    send_cap = max(2, (2 * BPR + lat - 1) // lat)
    blocks = -(-BPR * CELL // WIDTH)
    half_rows = blocks * 2 * channels
    padded_rows = -(-half_rows // LANES) * LANES
    turn_rows = -(-blocks // 8) * 8
    slot_rows = send_cap * channels
    select_rows = -(-lat * slot_rows // LANES) * LANES
    per_fld = pairs // fld
    dims = (lat, fld, pairs, slots, channels, degrees, group, send_cap, blocks)
    groups = slots // group
    waves = jnp.pad(wave_order.reshape(lat, slots), ((0, 0), (0, LANES - slots)))
    waves = jnp.roll(waves, position * group, 1)
    owner_rows = jnp.pad(
        owners.reshape(pairs, 2 * BPR), ((0, 0), (0, LANES - 2 * BPR)), constant_values=-1
    )
    anywhere = pl.BlockSpec(memory_space=pl.ANY)
    whole = pl.BlockSpec(memory_space=pltpu.VMEM)
    scalars = pl.BlockSpec(memory_space=pltpu.SMEM)
    received = pl.pallas_call(
        functools.partial(fused_kernel, dims),
        out_shape=jax.ShapeDtypeStruct((fld, per_fld, slot_rows, CELL), BF16),
        in_specs=[scalars, scalars, anywhere, anywhere, whole, whole],
        out_specs=anywhere,
        scratch_shapes=[
            pltpu.VMEM((2, slots * channels, degrees), BF16),
            pltpu.VMEM((slots * pairs, degrees), BF16),
            pltpu.VMEM((groups, 4 * channels, group * pairs), F32),
            pltpu.VMEM((pairs, 4 * channels, LANES), BF16),
            pltpu.VMEM((lat, 4 * channels, LANES), BF16),
            pltpu.VMEM((lat, WIDTH, 2 * LANES), BF16),
            pltpu.VMEM((lat, turn_rows, LANES), F32),
            pltpu.VMEM((lat, turn_rows, LANES), F32),
            pltpu.VMEM((half_rows, 2 * LANES), BF16),
            pltpu.VMEM((half_rows, WIDTH), F32),
            pltpu.VMEM((2 * padded_rows, CELL), BF16),
            pltpu.VMEM((select_rows, 2 * padded_rows), BF16),
            pltpu.VMEM((lat * slot_rows, CELL), BF16),
            pltpu.SemaphoreType.DMA((2, groups)),
            pltpu.SemaphoreType.DMA((lat,)),
            pltpu.SemaphoreType.DMA((lat,)),
            pltpu.SemaphoreType.DMA((lat,)),
            pltpu.SemaphoreType.DMA((fld, per_fld)),
            pltpu.SemaphoreType.DMA,
        ],
        compiler_params=pltpu.CompilerParams(
            collective_id=0, has_side_effects=True, vmem_limit_bytes=60000 * 1024
        ),
    )(
        wave_order,
        row_points,
        spectra.reshape(2, slots * channels, degrees),
        legendre.reshape(slots * pairs, degrees),
        waves,
        owner_rows,
    )
    split = received.reshape(fld, per_fld * send_cap, channels, CELL)
    return jnp.transpose(split, (1, 0, 2, 3)).reshape(per_fld * send_cap, fld * channels, CELL)


def solution(mesh):
    return jax.shard_map(
        functools.partial(on_device, mesh.shape["lat"], mesh.shape["fld"]),
        mesh=mesh,
        in_specs=(P(None, "lat", "fld", None), P("lat", None, None), P(), P(), P()),
        out_specs=P(("lat", "fld"), None, None),
        check_vma=False,
    )
```

```python
import functools
import math

import jax
import jax.numpy as jnp
from jax import lax
from jax.experimental import pallas as pl
from jax.experimental.pallas import tpu as pltpu
from jax.sharding import PartitionSpec as P

CELL = 128
BPR = 41
LANES = 128
WIDTH = 256
STEP = 16
MESH = pl.DeviceIdType.MESH
F32 = jnp.float32
BF16 = jnp.bfloat16
I32 = jnp.int32


def nt_dot(left, right):
    return lax.dot_general(left, right, (((1,), (1,)), ((), ())), preferred_element_type=F32)


def turn_tables(wave_row, index_column, points, inverse):
    product = wave_row * index_column
    remain = product - jnp.floor(product * inverse) * points
    remain = jnp.where(remain < 0, remain + points, remain)
    remain = jnp.where(remain >= points, remain - points, remain)
    quarter = jnp.floor(4.0 * remain * inverse + 0.5)
    angle = (4.0 * remain - quarter * points) * ((math.pi / 2) * inverse)
    square = angle * angle
    sine = angle * (
        1.0
        + square
        * (
            -1.0 / 6
            + square * (1.0 / 120 + square * (-1.0 / 5040 + square * (1.0 / 362880)))
        )
    )
    cosine = 1.0 + square * (
        -0.5
        + square
        * (
            1.0 / 24
            + square * (-1.0 / 720 + square * (1.0 / 40320 - square * (1.0 / 3628800)))
        )
    )
    swap = (quarter == 1.0) | (quarter == 3.0)
    cos_turned = jnp.where(swap, sine, cosine)
    sin_turned = jnp.where(swap, cosine, sine)
    cos_turned = jnp.where((quarter == 1.0) | (quarter == 2.0), -cos_turned, cos_turned)
    sin_turned = jnp.where((quarter == 2.0) | (quarter == 3.0), -sin_turned, sin_turned)
    return cos_turned, sin_turned


def fused_kernel(
    dims,
    waves_smem,
    points_smem,
    spectra_hbm,
    legendre_hbm,
    waves_ref,
    owners_ref,
    out_ref,
    spectra_buf,
    legendre_buf,
    permuted_buf,
    first_send,
    first_recv,
    basis_buf,
    turn_cos,
    turn_sin,
    rotated_buf,
    total_buf,
    grid_buf,
    select_buf,
    second_send,
    load_sems,
    send_sems1,
    recv_sems1,
    send_sems2,
    recv_sems2,
    local_sem,
    wave_buf,
    owner_buf,
):
    (lat, fld, pairs, slots, channels, degrees, group, send_cap, blocks) = dims
    groups = slots // group
    segments = LANES // group
    rows_s = group * channels
    rows_l = group * pairs
    half_rows = blocks * 2 * channels
    padded_rows = grid_buf.shape[0] // 2
    per_fld = pairs // fld
    slot_rows = send_cap * channels
    me = lax.axis_index("lat")
    my_fld = lax.axis_index("fld")
    home = lax.rem(me, fld)
    mine = me // fld
    my_pair = home * per_fld + mine

    barrier = pltpu.get_barrier_semaphore()
    everyone = lat * fld
    my_flat = me * fld + my_fld

    def greet(step, carry):
        other = lax.rem(my_flat + step, everyone)
        pl.semaphore_signal(
            barrier, inc=1, device_id=(other // fld, lax.rem(other, fld)), device_id_type=MESH
        )
        return carry

    def loads(index):
        row_s = pl.multiple_of(index * rows_s, rows_s)
        row_l = pl.multiple_of(index * rows_l, rows_l)
        return (
            pltpu.make_async_copy(
                spectra_hbm.at[:, pl.ds(row_s, rows_s), :],
                spectra_buf.at[:, pl.ds(row_s, rows_s), :],
                load_sems.at[0, index],
            ),
            pltpu.make_async_copy(
                legendre_hbm.at[pl.ds(row_l, rows_l), :],
                legendre_buf.at[pl.ds(row_l, rows_l), :],
                load_sems.at[1, index],
            ),
        )

    for index in range(groups):
        for copy in loads(index):
            copy.start()
    lax.fori_loop(1, everyone, greet, 0)

    degree = lax.broadcasted_iota(I32, (pairs, degrees), 1)
    alternate = (1 - 2 * (degree % 2)).astype(F32).astype(BF16)
    lane = lax.broadcasted_iota(I32, (channels, rows_l), 1)
    out_lane = lax.broadcasted_iota(I32, (8, rows_l), 1)
    in_row = lax.broadcasted_iota(I32, (rows_l, rows_l), 0)

    def legendre_group(index):
        for copy in loads(index):
            copy.wait()
        row_s = pl.multiple_of(index * rows_s, rows_s)
        row_l = pl.multiple_of(index * rows_l, rows_l)
        north_rows = []
        south_rows = []
        for slot in range(group):
            limit = degrees - waves_smem[me * slots + index * group + slot]
            keep = jnp.where(degree < limit, 1.0, 0.0).astype(F32).astype(BF16)
            table = legendre_buf[pl.ds(pl.multiple_of(row_l + slot * pairs, pairs), pairs), :] * keep
            north_rows.append(table)
            south_rows.append(table * alternate)
        values = jnp.concatenate(
            [spectra_buf[0, pl.ds(row_s, rows_s), :], spectra_buf[1, pl.ds(row_s, rows_s), :]], 0
        )
        summed = []
        for part in range(2):
            rows = north_rows if part == 0 else south_rows
            products = nt_dot(values, jnp.concatenate(rows, 0)).reshape(2, group, channels, rows_l)
            picked = []
            for part_of in range(2):
                kept = jnp.zeros((channels, rows_l), F32)
                for slot in range(group):
                    kept = jnp.where(lane // pairs == slot, products[part_of, slot], kept)
                picked.append(kept)
            summed.append(picked)
        stacked = jnp.concatenate([summed[0][0], summed[1][0], summed[0][1], summed[1][1]], 0)
        dest_half = out_lane // LANES
        segment = (out_lane % LANES) // group
        dest = dest_half * segments + lax.rem(segment - index + segments, segments)
        origin = ((out_lane % group) * pairs + dest)[:1]
        permute = (in_row == origin).astype(F32).astype(BF16)
        permuted_buf[index] = jnp.dot(stacked.astype(BF16), permute, preferred_element_type=F32)

    for index in range(groups):
        legendre_group(index)

    lane_segment = lax.broadcasted_iota(I32, (4 * channels, LANES), 1) // group
    for pair in range(pairs):
        at = (pair // segments) * LANES
        gathered = jnp.zeros((4 * channels, LANES), F32)
        for index in range(groups):
            gathered = jnp.where(
                lane_segment == (pair % segments + index) % segments,
                permuted_buf[index, :, at : at + LANES],
                gathered,
            )
        first_send[(pair % per_fld) * fld + pair // per_fld] = gathered.astype(BF16)

    pl.semaphore_wait(barrier, everyone - 1)

    def first_copy(step):
        other = lax.rem(me + step, lat)
        return pltpu.make_async_remote_copy(
            src_ref=first_send.at[other],
            dst_ref=first_recv.at[me],
            send_sem=send_sems1.at[step],
            recv_sem=recv_sems1.at[step],
            device_id=(other, my_fld),
            device_id_type=MESH,
        )

    def first_start(step, carry):
        first_copy(step).start()
        return carry

    lax.fori_loop(1, lat, first_start, 0)

    points = jnp.full((1, LANES), points_smem[my_pair], I32).astype(F32)
    inverse = 1.0 / points

    def window_of(buffer, start):
        aligned = start // LANES * LANES
        chunk = buffer[:, pl.ds(pl.multiple_of(aligned, LANES), 2 * LANES)]
        chunk = jnp.broadcast_to(chunk, (8, 2 * LANES))
        return pltpu.roll(chunk, lax.rem(2 * LANES - (start - aligned), 2 * LANES), 1)[:, :LANES]

    table_rows = turn_cos.shape[1] + 2 * STEP
    row_index = lax.broadcasted_iota(I32, (table_rows, LANES), 0)
    index_column = jnp.where(
        row_index < STEP,
        row_index,
        jnp.where(row_index < 2 * STEP, (row_index - STEP) * STEP, (row_index - 2 * STEP) * WIDTH),
    ).astype(F32)

    wave_buf[...] = jnp.zeros(wave_buf.shape, I32)
    wave_buf[:, : waves_ref.shape[1]] = waves_ref[...]

    def make_tables(source, carry):
        wave_row = window_of(wave_buf, source * slots)
        wave_row = pltpu.roll(wave_row, lax.rem(my_pair, segments) * group, 1)[:1]
        cos_all, sin_all = turn_tables(wave_row.astype(F32), index_column, points, inverse)
        weight = jnp.where(wave_row == 0, 1.0, 2.0).astype(F32)
        turn_cos[source] = cos_all[2 * STEP :] * weight
        turn_sin[source] = sin_all[2 * STEP :] * weight
        cos_low, sin_low = cos_all[:STEP], sin_all[:STEP]
        for high in range(WIDTH // STEP):
            cos_high = cos_all[STEP + high : STEP + high + 1]
            sin_high = sin_all[STEP + high : STEP + high + 1]
            place = slice(high * STEP, (high + 1) * STEP)
            basis_buf[source, place, :LANES] = (cos_high * cos_low - sin_high * sin_low).astype(BF16)
            basis_buf[source, place, LANES:] = (sin_high * cos_low + cos_high * sin_low).astype(BF16)
        return carry

    lax.fori_loop(0, lat, make_tables, 0)

    owner_buf[...] = jnp.zeros(owner_buf.shape, I32)
    owner_buf[:, : owners_ref.shape[1]] = owners_ref[...]
    owner_row = window_of(owner_buf, my_pair * 2 * BPR)[:1]
    owner_row = jnp.where(lax.broadcasted_iota(I32, (1, LANES), 1) < 2 * BPR, owner_row, -1)
    onehot = (lax.broadcasted_iota(I32, (lat, LANES), 0) == owner_row).astype(F32)
    upper = (
        lax.broadcasted_iota(I32, (LANES, LANES), 0) < lax.broadcasted_iota(I32, (LANES, LANES), 1)
    ).astype(F32)
    earlier = jnp.dot(onehot.astype(BF16), upper.astype(BF16), preferred_element_type=F32)
    rank_row = jnp.sum(onehot * earlier, axis=0, keepdims=True)
    which = lax.broadcasted_iota(I32, (16, LANES), 0)
    both = jnp.where(which == 0, owner_row.astype(F32), jnp.where(which == 1, rank_row, 0.0))
    total_columns = 2 * padded_rows
    column = lax.broadcasted_iota(I32, (8, total_columns), 1)
    half = column // padded_rows
    inner = column - half * padded_rows
    span = inner // (2 * channels)
    mirror = (inner // channels) % 2
    block = 2 * span + half
    valid = (inner < half_rows) & (block < BPR)
    number = jnp.where(valid, mirror * BPR + block, -1)[:1]
    expand = (lax.broadcasted_iota(I32, (LANES, total_columns), 0) == number).astype(F32)
    spread = jnp.dot(both.astype(BF16), expand.astype(BF16), preferred_element_type=F32)
    spread = spread.astype(I32)
    channel = column[:1] % channels
    target = spread[0:1] * slot_rows + spread[1:2] * channels + channel
    target = jnp.where(valid[:1], target, -1)

    def make_select(index, carry):
        start = pl.multiple_of(index * LANES, LANES)
        rows = lax.broadcasted_iota(I32, (LANES, total_columns), 0) + start
        select_buf[pl.ds(start, LANES), :] = (rows == target).astype(F32).astype(BF16)
        return carry

    lax.fori_loop(0, select_buf.shape[0] // LANES, make_select, 0)

    def accumulate(source, arrived, place_of):
        real = arrived[: 2 * channels].astype(F32)
        imag = arrived[2 * channels :].astype(F32)
        cos_rows = turn_cos[source]
        sin_rows = turn_sin[source]
        for span_index in range(blocks):
            cos_turn = cos_rows[span_index : span_index + 1]
            sin_turn = sin_rows[span_index : span_index + 1]
            place = slice(span_index * 2 * channels, (span_index + 1) * 2 * channels)
            rotated_buf[place_of, place, :LANES] = (real * cos_turn - imag * sin_turn).astype(BF16)
            rotated_buf[place_of, place, LANES:] = (-(real * sin_turn + imag * cos_turn)).astype(BF16)
        return nt_dot(rotated_buf[place_of], basis_buf[source])

    total_buf[...] = accumulate(me, first_send[me], 0)
    unrolled = rotated_buf.shape[0]

    def arrive(turn, carry):
        steps = [1 + turn * unrolled + within for within in range(unrolled)]
        for step in steps:
            first_copy(step).wait_recv()
        product = None
        for within, step in enumerate(steps):
            source = lax.rem(me + lat - step, lat)
            term = accumulate(source, first_recv[source], within)
            product = term if product is None else product + term
        total_buf[...] += product
        return carry

    lax.fori_loop(0, (lat - 1) // unrolled, arrive, 0)

    grid_buf[...] = jnp.zeros(grid_buf.shape, BF16)
    offset = lax.broadcasted_iota(I32, (2 * channels, WIDTH), 1)
    for span_index in range(blocks):
        low, high = span_index * 2 * channels, (span_index + 1) * 2 * channels
        inside = offset < points_smem[my_pair] - span_index * WIDTH
        grid = jnp.where(inside, total_buf[low:high], 0.0).astype(BF16)
        grid_buf[low:high, :] = grid[:, :CELL]
        grid_buf[padded_rows + low : padded_rows + high, :] = grid[:, CELL:]
    routed = jnp.dot(select_buf[...], grid_buf[...], preferred_element_type=F32).astype(BF16)
    second_send[...] = routed[: lat * slot_rows]

    def second_copy(step):
        other = lax.rem(me + step, lat)
        return pltpu.make_async_remote_copy(
            src_ref=second_send.at[pl.ds(pl.multiple_of(other * slot_rows, slot_rows), slot_rows), :],
            dst_ref=out_ref.at[my_fld, mine],
            send_sem=send_sems2.at[step],
            recv_sem=recv_sems2.at[my_fld, mine],
            device_id=(other, home),
            device_id_type=MESH,
        )

    own_copy = pltpu.make_async_copy(
        second_send.at[pl.ds(pl.multiple_of(me * slot_rows, slot_rows), slot_rows), :],
        out_ref.at[my_fld, mine],
        local_sem,
    )

    def second_start(step, carry):
        second_copy(step).start()
        return carry

    lax.fori_loop(1, lat, second_start, 0)

    @pl.when(home == my_fld)
    def _():
        own_copy.start()

    @pl.when(home != my_fld)
    def _():
        second_copy(0).start()

    def first_done(step, carry):
        first_copy(step).wait_send()
        return carry

    lax.fori_loop(1, lat, first_done, 0)

    def second_done(step, carry):
        second_copy(step).wait_send()
        return carry

    lax.fori_loop(1, lat, second_done, 0)

    @pl.when(home == my_fld)
    def _():
        own_copy.wait()

    @pl.when(home != my_fld)
    def _():
        second_copy(0).wait_send()

    def from_source(step, carry):
        from_fld = step // per_fld
        from_pair = lax.rem(step, per_fld)
        is_self = (from_fld == my_fld) & (from_pair * fld + my_fld == me)

        @pl.when(jnp.logical_not(is_self))
        def _():
            pltpu.make_async_remote_copy(
                src_ref=second_send.at[pl.ds(0, slot_rows), :],
                dst_ref=out_ref.at[from_fld, from_pair],
                send_sem=send_sems2.at[0],
                recv_sem=recv_sems2.at[from_fld, from_pair],
                device_id=(me, my_fld),
                device_id_type=MESH,
            ).wait_recv()

        return carry

    lax.fori_loop(0, fld * per_fld, from_source, 0)


def on_device(lat, fld, spectra, legendre, wave_order, row_points, owners):
    slots, pairs, degrees = legendre.shape
    channels = spectra.shape[2]
    group = max(g for g in range(1, slots + 1) if slots % g == 0 and g * pairs <= 256 and LANES % g == 0)
    send_cap = max(2, (2 * BPR + lat - 1) // lat)
    blocks = -(-BPR * CELL // WIDTH)
    half_rows = blocks * 2 * channels
    padded_rows = -(-half_rows // LANES) * LANES
    turn_rows = -(-blocks // 8) * 8
    slot_rows = send_cap * channels
    select_rows = -(-lat * slot_rows // LANES) * LANES
    per_fld = pairs // fld
    dims = (lat, fld, pairs, slots, channels, degrees, group, send_cap, blocks)
    groups = slots // group
    unrolled = max(u for u in range(1, 6) if (lat - 1) % u == 0)
    anywhere = pl.BlockSpec(memory_space=pl.ANY)
    whole = pl.BlockSpec(memory_space=pltpu.VMEM)
    scalars = pl.BlockSpec(memory_space=pltpu.SMEM)
    received = pl.pallas_call(
        functools.partial(fused_kernel, dims),
        out_shape=jax.ShapeDtypeStruct((fld, per_fld, slot_rows, CELL), BF16),
        in_specs=[scalars, scalars, anywhere, anywhere, whole, whole],
        out_specs=anywhere,
        scratch_shapes=[
            pltpu.VMEM((2, slots * channels, degrees), BF16),
            pltpu.VMEM((slots * pairs, degrees), BF16),
            pltpu.VMEM((groups, 4 * channels, group * pairs), F32),
            pltpu.VMEM((pairs, 4 * channels, LANES), BF16),
            pltpu.VMEM((lat, 4 * channels, LANES), BF16),
            pltpu.VMEM((lat, WIDTH, 2 * LANES), BF16),
            pltpu.VMEM((lat, turn_rows, LANES), F32),
            pltpu.VMEM((lat, turn_rows, LANES), F32),
            pltpu.VMEM((unrolled, half_rows, 2 * LANES), BF16),
            pltpu.VMEM((half_rows, WIDTH), F32),
            pltpu.VMEM((2 * padded_rows, CELL), BF16),
            pltpu.VMEM((select_rows, 2 * padded_rows), BF16),
            pltpu.VMEM((lat * slot_rows, CELL), BF16),
            pltpu.SemaphoreType.DMA((2, groups)),
            pltpu.SemaphoreType.DMA((lat,)),
            pltpu.SemaphoreType.DMA((lat,)),
            pltpu.SemaphoreType.DMA((lat,)),
            pltpu.SemaphoreType.DMA((fld, per_fld)),
            pltpu.SemaphoreType.DMA,
            pltpu.VMEM((1, -(-wave_order.shape[0] // LANES) * LANES + 2 * LANES), I32),
            pltpu.VMEM((1, -(-owners.shape[0] // LANES) * LANES + 2 * LANES), I32),
        ],
        compiler_params=pltpu.CompilerParams(
            collective_id=0, has_side_effects=True, vmem_limit_bytes=60000 * 1024
        ),
    )(
        wave_order,
        row_points,
        spectra.reshape(2, slots * channels, degrees),
        legendre.reshape(slots * pairs, degrees),
        wave_order.reshape(1, lat * slots),
        owners.reshape(1, pairs * 2 * BPR),
    )
    split = received.reshape(fld, per_fld * send_cap, channels, CELL)
    return jnp.transpose(split, (1, 0, 2, 3)).reshape(per_fld * send_cap, fld * channels, CELL)


def solution(mesh):
    return jax.shard_map(
        functools.partial(on_device, mesh.shape["lat"], mesh.shape["fld"]),
        mesh=mesh,
        in_specs=(P(None, "lat", "fld", None), P("lat", None, None), P(), P(), P()),
        out_specs=P(("lat", "fld"), None, None),
        check_vma=False,
    )
```

```python
import functools
import math

import jax
import jax.numpy as jnp
from jax import lax
from jax.experimental import pallas as pl
from jax.experimental.pallas import tpu as pltpu
from jax.sharding import PartitionSpec as P

CELL = 128
BPR = 41
LANES = 128
WIDTH = 256
STEP = 16
MESH = pl.DeviceIdType.MESH
F32 = jnp.float32
BF16 = jnp.bfloat16
I32 = jnp.int32


def nt_dot(left, right):
    return lax.dot_general(left, right, (((1,), (1,)), ((), ())), preferred_element_type=F32)


def turn_tables(wave_row, index_column, points, inverse):
    product = wave_row * index_column
    remain = product - jnp.floor(product * inverse) * points
    remain = jnp.where(remain < 0, remain + points, remain)
    remain = jnp.where(remain >= points, remain - points, remain)
    quarter = jnp.floor(4.0 * remain * inverse + 0.5)
    angle = (4.0 * remain - quarter * points) * ((math.pi / 2) * inverse)
    square = angle * angle
    sine = angle * (
        1.0
        + square
        * (
            -1.0 / 6
            + square * (1.0 / 120 + square * (-1.0 / 5040 + square * (1.0 / 362880)))
        )
    )
    cosine = 1.0 + square * (
        -0.5
        + square
        * (
            1.0 / 24
            + square * (-1.0 / 720 + square * (1.0 / 40320 - square * (1.0 / 3628800)))
        )
    )
    swap = (quarter == 1.0) | (quarter == 3.0)
    cos_turned = jnp.where(swap, sine, cosine)
    sin_turned = jnp.where(swap, cosine, sine)
    cos_turned = jnp.where((quarter == 1.0) | (quarter == 2.0), -cos_turned, cos_turned)
    sin_turned = jnp.where((quarter == 2.0) | (quarter == 3.0), -sin_turned, sin_turned)
    return cos_turned, sin_turned


def fused_kernel(
    dims,
    waves_hbm,
    points_hbm,
    spectra_hbm,
    legendre_hbm,
    owners_hbm,
    out_ref,
    spectra_buf,
    legendre_buf,
    permuted_buf,
    first_send,
    first_recv,
    basis_buf,
    turn_cos,
    turn_sin,
    rotated_buf,
    total_buf,
    grid_buf,
    select_buf,
    second_send,
    load_sems,
    send_sems1,
    recv_sems1,
    send_sems2,
    recv_sems2,
    local_sem,
    wave_buf,
    owner_buf,
    waves_smem,
    points_smem,
    waves_ref,
    owners_ref,
    small_sems,
):
    (lat, fld, pairs, slots, channels, degrees, group, send_cap, blocks) = dims
    groups = slots // group
    segments = LANES // group
    rows_s = group * channels
    rows_l = group * pairs
    half_rows = blocks * 2 * channels
    padded_rows = grid_buf.shape[0] // 2
    per_fld = pairs // fld
    slot_rows = send_cap * channels
    me = lax.axis_index("lat")
    my_fld = lax.axis_index("fld")
    home = lax.rem(me, fld)
    mine = me // fld
    my_pair = home * per_fld + mine

    barrier = pltpu.get_barrier_semaphore()
    everyone = lat * fld
    my_flat = me * fld + my_fld

    def greet(step, carry):
        other = lax.rem(my_flat + step, everyone)
        pl.semaphore_signal(
            barrier, inc=1, device_id=(other // fld, lax.rem(other, fld)), device_id_type=MESH
        )
        return carry

    def loads(index):
        row_s = pl.multiple_of(index * rows_s, rows_s)
        row_l = pl.multiple_of(index * rows_l, rows_l)
        return (
            pltpu.make_async_copy(
                spectra_hbm.at[:, pl.ds(row_s, rows_s), :],
                spectra_buf.at[:, pl.ds(row_s, rows_s), :],
                load_sems.at[0, index],
            ),
            pltpu.make_async_copy(
                legendre_hbm.at[pl.ds(row_l, rows_l), :],
                legendre_buf.at[pl.ds(row_l, rows_l), :],
                load_sems.at[1, index],
            ),
        )

    small = [
        pltpu.make_async_copy(source, target, small_sems.at[number])
        for number, (source, target) in enumerate(
            [
                (waves_hbm, waves_smem),
                (points_hbm, points_smem),
                (waves_hbm, waves_ref),
                (owners_hbm, owners_ref),
            ]
        )
    ]
    for copy in small:
        copy.start()
    for index in range(groups):
        for copy in loads(index):
            copy.start()
    lax.fori_loop(1, everyone, greet, 0)
    for copy in small:
        copy.wait()

    degree = lax.broadcasted_iota(I32, (pairs, degrees), 1)
    alternate = (1 - 2 * (degree % 2)).astype(F32).astype(BF16)
    lane = lax.broadcasted_iota(I32, (channels, rows_l), 1)
    out_lane = lax.broadcasted_iota(I32, (8, rows_l), 1)
    in_row = lax.broadcasted_iota(I32, (rows_l, rows_l), 0)

    def legendre_group(index):
        for copy in loads(index):
            copy.wait()
        row_s = pl.multiple_of(index * rows_s, rows_s)
        row_l = pl.multiple_of(index * rows_l, rows_l)
        north_rows = []
        south_rows = []
        for slot in range(group):
            limit = degrees - waves_smem[me * slots + index * group + slot]
            keep = jnp.where(degree < limit, 1.0, 0.0).astype(F32).astype(BF16)
            table = legendre_buf[pl.ds(pl.multiple_of(row_l + slot * pairs, pairs), pairs), :] * keep
            north_rows.append(table)
            south_rows.append(table * alternate)
        values = jnp.concatenate(
            [spectra_buf[0, pl.ds(row_s, rows_s), :], spectra_buf[1, pl.ds(row_s, rows_s), :]], 0
        )
        summed = []
        for part in range(2):
            rows = north_rows if part == 0 else south_rows
            products = nt_dot(values, jnp.concatenate(rows, 0)).reshape(2, group, channels, rows_l)
            picked = []
            for part_of in range(2):
                kept = jnp.zeros((channels, rows_l), F32)
                for slot in range(group):
                    kept = jnp.where(lane // pairs == slot, products[part_of, slot], kept)
                picked.append(kept)
            summed.append(picked)
        stacked = jnp.concatenate([summed[0][0], summed[1][0], summed[0][1], summed[1][1]], 0)
        dest_half = out_lane // LANES
        segment = (out_lane % LANES) // group
        dest = dest_half * segments + lax.rem(segment - index + segments, segments)
        origin = ((out_lane % group) * pairs + dest)[:1]
        permute = (in_row == origin).astype(F32).astype(BF16)
        permuted_buf[index] = jnp.dot(stacked.astype(BF16), permute, preferred_element_type=F32)

    for index in range(groups):
        legendre_group(index)

    lane_segment = lax.broadcasted_iota(I32, (4 * channels, LANES), 1) // group
    for pair in range(pairs):
        at = (pair // segments) * LANES
        gathered = jnp.zeros((4 * channels, LANES), F32)
        for index in range(groups):
            gathered = jnp.where(
                lane_segment == (pair % segments + index) % segments,
                permuted_buf[index, :, at : at + LANES],
                gathered,
            )
        first_send[(pair % per_fld) * fld + pair // per_fld] = gathered.astype(BF16)

    pl.semaphore_wait(barrier, everyone - 1)

    def first_copy(step):
        other = lax.rem(me + step, lat)
        return pltpu.make_async_remote_copy(
            src_ref=first_send.at[other],
            dst_ref=first_recv.at[me],
            send_sem=send_sems1.at[step],
            recv_sem=recv_sems1.at[step],
            device_id=(other, my_fld),
            device_id_type=MESH,
        )

    def first_start(step, carry):
        first_copy(step).start()
        return carry

    lax.fori_loop(1, lat, first_start, 0)

    points = jnp.full((1, LANES), points_smem[my_pair], I32).astype(F32)
    inverse = 1.0 / points

    def window_of(buffer, start):
        aligned = start // LANES * LANES
        chunk = buffer[:, pl.ds(pl.multiple_of(aligned, LANES), 2 * LANES)]
        chunk = jnp.broadcast_to(chunk, (8, 2 * LANES))
        return pltpu.roll(chunk, lax.rem(2 * LANES - (start - aligned), 2 * LANES), 1)[:, :LANES]

    table_rows = turn_cos.shape[1] + 2 * STEP
    row_index = lax.broadcasted_iota(I32, (table_rows, LANES), 0)
    index_column = jnp.where(
        row_index < STEP,
        row_index,
        jnp.where(row_index < 2 * STEP, (row_index - STEP) * STEP, (row_index - 2 * STEP) * WIDTH),
    ).astype(F32)

    wave_buf[...] = jnp.zeros(wave_buf.shape, I32)
    wave_buf[:, : lat * slots] = waves_ref[...].reshape(1, lat * slots)

    def make_tables(source, carry):
        wave_row = window_of(wave_buf, source * slots)
        wave_row = pltpu.roll(wave_row, lax.rem(my_pair, segments) * group, 1)[:1]
        cos_all, sin_all = turn_tables(wave_row.astype(F32), index_column, points, inverse)
        weight = jnp.where(wave_row == 0, 1.0, 2.0).astype(F32)
        turn_cos[source] = cos_all[2 * STEP :] * weight
        turn_sin[source] = sin_all[2 * STEP :] * weight
        cos_low, sin_low = cos_all[:STEP], sin_all[:STEP]
        for high in range(WIDTH // STEP):
            cos_high = cos_all[STEP + high : STEP + high + 1]
            sin_high = sin_all[STEP + high : STEP + high + 1]
            place = slice(high * STEP, (high + 1) * STEP)
            basis_buf[source, place, :LANES] = (cos_high * cos_low - sin_high * sin_low).astype(BF16)
            basis_buf[source, place, LANES:] = (sin_high * cos_low + cos_high * sin_low).astype(BF16)
        return carry

    lax.fori_loop(0, lat, make_tables, 0, unroll=4 if lat % 4 == 0 else 1)

    owner_buf[...] = jnp.zeros(owner_buf.shape, I32)
    owner_buf[:, : owners_ref.shape[1]] = owners_ref[...]
    owner_row = window_of(owner_buf, my_pair * 2 * BPR)[:1]
    owner_row = jnp.where(lax.broadcasted_iota(I32, (1, LANES), 1) < 2 * BPR, owner_row, -1)
    onehot = (lax.broadcasted_iota(I32, (lat, LANES), 0) == owner_row).astype(F32)
    upper = (
        lax.broadcasted_iota(I32, (LANES, LANES), 0) < lax.broadcasted_iota(I32, (LANES, LANES), 1)
    ).astype(F32)
    earlier = jnp.dot(onehot.astype(BF16), upper.astype(BF16), preferred_element_type=F32)
    rank_row = jnp.sum(onehot * earlier, axis=0, keepdims=True)
    which = lax.broadcasted_iota(I32, (16, LANES), 0)
    both = jnp.where(which == 0, owner_row.astype(F32), jnp.where(which == 1, rank_row, 0.0))
    total_columns = 2 * padded_rows
    column = lax.broadcasted_iota(I32, (8, total_columns), 1)
    half = column // padded_rows
    inner = column - half * padded_rows
    span = inner // (2 * channels)
    mirror = (inner // channels) % 2
    block = 2 * span + half
    valid = (inner < half_rows) & (block < BPR)
    number = jnp.where(valid, mirror * BPR + block, -1)[:1]
    expand = (lax.broadcasted_iota(I32, (LANES, total_columns), 0) == number).astype(F32)
    spread = jnp.dot(both.astype(BF16), expand.astype(BF16), preferred_element_type=F32)
    spread = spread.astype(I32)
    channel = column[:1] % channels
    target = spread[0:1] * slot_rows + spread[1:2] * channels + channel
    target = jnp.where(valid[:1], target, -1)

    def make_select(index, carry):
        start = pl.multiple_of(index * LANES, LANES)
        rows = lax.broadcasted_iota(I32, (LANES, total_columns), 0) + start
        select_buf[pl.ds(start, LANES), :] = (rows == target).astype(F32).astype(BF16)
        return carry

    lax.fori_loop(0, select_buf.shape[0] // LANES, make_select, 0)

    def accumulate(source, arrived, place_of):
        real = arrived[: 2 * channels].astype(F32)
        imag = arrived[2 * channels :].astype(F32)
        cos_rows = turn_cos[source]
        sin_rows = turn_sin[source]
        for span_index in range(blocks):
            cos_turn = cos_rows[span_index : span_index + 1]
            sin_turn = sin_rows[span_index : span_index + 1]
            place = slice(span_index * 2 * channels, (span_index + 1) * 2 * channels)
            rotated_buf[place_of, place, :LANES] = (real * cos_turn - imag * sin_turn).astype(BF16)
            rotated_buf[place_of, place, LANES:] = (-(real * sin_turn + imag * cos_turn)).astype(BF16)
        return nt_dot(rotated_buf[place_of], basis_buf[source])

    total_buf[...] = accumulate(me, first_send[me], 0)
    unrolled = rotated_buf.shape[0]

    def arrive(turn, carry):
        steps = [1 + turn * unrolled + within for within in range(unrolled)]
        for step in steps:
            first_copy(step).wait_recv()
        product = None
        for within, step in enumerate(steps):
            source = lax.rem(me + lat - step, lat)
            term = accumulate(source, first_recv[source], within)
            product = term if product is None else product + term
        total_buf[...] += product
        return carry

    lax.fori_loop(0, (lat - 1) // unrolled, arrive, 0)

    grid_buf[...] = jnp.zeros(grid_buf.shape, BF16)
    offset = lax.broadcasted_iota(I32, (2 * channels, WIDTH), 1)
    for span_index in range(blocks):
        low, high = span_index * 2 * channels, (span_index + 1) * 2 * channels
        inside = offset < points_smem[my_pair] - span_index * WIDTH
        grid = jnp.where(inside, total_buf[low:high], 0.0).astype(BF16)
        grid_buf[low:high, :] = grid[:, :CELL]
        grid_buf[padded_rows + low : padded_rows + high, :] = grid[:, CELL:]

    def second_copy(step):
        other = lax.rem(me + step, lat)
        return pltpu.make_async_remote_copy(
            src_ref=second_send.at[pl.ds(pl.multiple_of(other * slot_rows, slot_rows), slot_rows), :],
            dst_ref=out_ref.at[my_fld, mine],
            send_sem=send_sems2.at[step],
            recv_sem=recv_sems2.at[my_fld, mine],
            device_id=(other, home),
            device_id_type=MESH,
        )

    own_copy = pltpu.make_async_copy(
        second_send.at[pl.ds(pl.multiple_of(me * slot_rows, slot_rows), slot_rows), :],
        out_ref.at[my_fld, mine],
        local_sem,
    )

    together = 4 if lat % 4 == 0 else 1
    chunks = lat // together
    chunk_rows = together * slot_rows
    for turn in range(chunks):
        chunk = lax.rem(me // together + turn, chunks)
        rows = pl.ds(pl.multiple_of(chunk * chunk_rows, chunk_rows), chunk_rows)
        second_send[rows, :] = jnp.dot(
            select_buf[rows, :], grid_buf[...], preferred_element_type=F32
        ).astype(BF16)
        for within in range(together):
            step = lax.rem(chunk * together + within + lat - me, lat)
            stays = (step == 0) & (home == my_fld)

            @pl.when(stays)
            def _():
                own_copy.start()

            @pl.when(jnp.logical_not(stays))
            def _():
                second_copy(step).start()

    def first_done(step, carry):
        first_copy(step).wait_send()
        return carry

    lax.fori_loop(1, lat, first_done, 0)

    def second_done(step, carry):
        second_copy(step).wait_send()
        return carry

    lax.fori_loop(1, lat, second_done, 0)

    @pl.when(home == my_fld)
    def _():
        own_copy.wait()

    @pl.when(home != my_fld)
    def _():
        second_copy(0).wait_send()

    def from_source(step, carry):
        from_fld = step // per_fld
        from_pair = lax.rem(step, per_fld)
        is_self = (from_fld == my_fld) & (from_pair * fld + my_fld == me)

        @pl.when(jnp.logical_not(is_self))
        def _():
            pltpu.make_async_remote_copy(
                src_ref=second_send.at[pl.ds(0, slot_rows), :],
                dst_ref=out_ref.at[from_fld, from_pair],
                send_sem=send_sems2.at[0],
                recv_sem=recv_sems2.at[from_fld, from_pair],
                device_id=(me, my_fld),
                device_id_type=MESH,
            ).wait_recv()

        return carry

    lax.fori_loop(0, fld * per_fld, from_source, 0)


def on_device(lat, fld, spectra, legendre, wave_order, row_points, owners):
    slots, pairs, degrees = legendre.shape
    channels = spectra.shape[2]
    group = max(g for g in range(1, slots + 1) if slots % g == 0 and g * pairs <= 256 and LANES % g == 0)
    send_cap = max(2, (2 * BPR + lat - 1) // lat)
    blocks = -(-BPR * CELL // WIDTH)
    half_rows = blocks * 2 * channels
    padded_rows = -(-half_rows // LANES) * LANES
    turn_rows = -(-blocks // 8) * 8
    slot_rows = send_cap * channels
    select_rows = -(-lat * slot_rows // LANES) * LANES
    per_fld = pairs // fld
    dims = (lat, fld, pairs, slots, channels, degrees, group, send_cap, blocks)
    groups = slots // group
    unrolled = max(u for u in range(1, 6) if (lat - 1) % u == 0)
    anywhere = pl.BlockSpec(memory_space=pl.ANY)
    received = pl.pallas_call(
        functools.partial(fused_kernel, dims),
        out_shape=jax.ShapeDtypeStruct((fld, per_fld, slot_rows, CELL), BF16),
        in_specs=[anywhere] * 5,
        out_specs=anywhere,
        scratch_shapes=[
            pltpu.VMEM((2, slots * channels, degrees), BF16),
            pltpu.VMEM((slots * pairs, degrees), BF16),
            pltpu.VMEM((groups, 4 * channels, group * pairs), F32),
            pltpu.VMEM((pairs, 4 * channels, LANES), BF16),
            pltpu.VMEM((lat, 4 * channels, LANES), BF16),
            pltpu.VMEM((lat, WIDTH, 2 * LANES), BF16),
            pltpu.VMEM((lat, turn_rows, LANES), F32),
            pltpu.VMEM((lat, turn_rows, LANES), F32),
            pltpu.VMEM((unrolled, half_rows, 2 * LANES), BF16),
            pltpu.VMEM((half_rows, WIDTH), F32),
            pltpu.VMEM((2 * padded_rows, CELL), BF16),
            pltpu.VMEM((select_rows, 2 * padded_rows), BF16),
            pltpu.VMEM((lat * slot_rows, CELL), BF16),
            pltpu.SemaphoreType.DMA((2, groups)),
            pltpu.SemaphoreType.DMA((lat,)),
            pltpu.SemaphoreType.DMA((lat,)),
            pltpu.SemaphoreType.DMA((lat,)),
            pltpu.SemaphoreType.DMA((fld, per_fld)),
            pltpu.SemaphoreType.DMA,
            pltpu.VMEM((1, -(-wave_order.shape[0] // LANES) * LANES + 2 * LANES), I32),
            pltpu.VMEM((1, -(-owners.shape[0] // LANES) * LANES + 2 * LANES), I32),
            pltpu.SMEM(wave_order.shape, I32),
            pltpu.SMEM(row_points.shape, I32),
            pltpu.VMEM(wave_order.shape, I32),
            pltpu.VMEM((1, owners.shape[0]), I32),
            pltpu.SemaphoreType.DMA((4,)),
        ],
        compiler_params=pltpu.CompilerParams(
            collective_id=0, has_side_effects=True, vmem_limit_bytes=60000 * 1024
        ),
    )(
        wave_order,
        row_points,
        spectra.reshape(2, slots * channels, degrees),
        legendre.reshape(slots * pairs, degrees),
        owners.reshape(1, pairs * 2 * BPR),
    )
    split = received.reshape(fld, per_fld * send_cap, channels, CELL)
    return jnp.transpose(split, (1, 0, 2, 3)).reshape(per_fld * send_cap, fld * channels, CELL)


def solution(mesh):
    return jax.shard_map(
        functools.partial(on_device, mesh.shape["lat"], mesh.shape["fld"]),
        mesh=mesh,
        in_specs=(P(None, "lat", "fld", None), P("lat", None, None), P(), P(), P()),
        out_specs=P(("lat", "fld"), None, None),
        check_vma=False,
    )
```

```python
import functools
import math

import jax
import jax.numpy as jnp
from jax import lax
from jax.experimental import pallas as pl
from jax.experimental.pallas import tpu as pltpu
from jax.sharding import PartitionSpec as P

CELL = 128
BPR = 41
LANES = 128
WIDTH = 256
STEP = 16
MESH = pl.DeviceIdType.MESH
F32 = jnp.float32
BF16 = jnp.bfloat16
I32 = jnp.int32


def nt_dot(left, right):
    return lax.dot_general(left, right, (((1,), (1,)), ((), ())), preferred_element_type=F32)


def turn_tables(wave_row, index_column, points, inverse):
    product = wave_row * index_column
    remain = product - jnp.floor(product * inverse) * points
    remain = jnp.where(remain < 0, remain + points, remain)
    remain = jnp.where(remain >= points, remain - points, remain)
    quarter = jnp.floor(4.0 * remain * inverse + 0.5)
    angle = (4.0 * remain - quarter * points) * ((math.pi / 2) * inverse)
    square = angle * angle
    sine = angle * (
        1.0
        + square
        * (
            -1.0 / 6
            + square * (1.0 / 120 + square * (-1.0 / 5040 + square * (1.0 / 362880)))
        )
    )
    cosine = 1.0 + square * (
        -0.5
        + square
        * (
            1.0 / 24
            + square * (-1.0 / 720 + square * (1.0 / 40320 - square * (1.0 / 3628800)))
        )
    )
    swap = (quarter == 1.0) | (quarter == 3.0)
    cos_turned = jnp.where(swap, sine, cosine)
    sin_turned = jnp.where(swap, cosine, sine)
    cos_turned = jnp.where((quarter == 1.0) | (quarter == 2.0), -cos_turned, cos_turned)
    sin_turned = jnp.where((quarter == 2.0) | (quarter == 3.0), -sin_turned, sin_turned)
    return cos_turned, sin_turned


def fused_kernel(
    dims,
    waves_hbm,
    points_hbm,
    spectra_hbm,
    legendre_hbm,
    owners_hbm,
    out_ref,
    spectra_buf,
    legendre_buf,
    permuted_buf,
    first_send,
    first_recv,
    basis_buf,
    turn_cos,
    turn_sin,
    rotated_buf,
    total_buf,
    grid_buf,
    select_buf,
    second_send,
    load_sems,
    send_sems1,
    recv_sems1,
    send_sems2,
    recv_sems2,
    local_sem,
    wave_buf,
    owner_buf,
    waves_smem,
    points_smem,
    waves_ref,
    owners_ref,
    small_sems,
):
    (lat, fld, pairs, slots, channels, degrees, group, send_cap, blocks) = dims
    groups = slots // group
    segments = LANES // group
    rows_s = group * channels
    rows_l = group * pairs
    half_rows = blocks * 2 * channels
    padded_rows = grid_buf.shape[0] // 2
    per_fld = pairs // fld
    slot_rows = send_cap * channels
    me = lax.axis_index("lat")
    my_fld = lax.axis_index("fld")
    home = lax.rem(me, fld)
    mine = me // fld
    my_pair = home * per_fld + mine

    barrier = pltpu.get_barrier_semaphore()
    everyone = lat * fld
    my_flat = me * fld + my_fld

    def greet(step, carry):
        other = lax.rem(my_flat + step, everyone)
        pl.semaphore_signal(
            barrier, inc=1, device_id=(other // fld, lax.rem(other, fld)), device_id_type=MESH
        )
        return carry

    def loads(index):
        row_s = pl.multiple_of(index * rows_s, rows_s)
        row_l = pl.multiple_of(index * rows_l, rows_l)
        return (
            pltpu.make_async_copy(
                spectra_hbm.at[:, pl.ds(row_s, rows_s), :],
                spectra_buf.at[:, pl.ds(row_s, rows_s), :],
                load_sems.at[0, index],
            ),
            pltpu.make_async_copy(
                legendre_hbm.at[pl.ds(row_l, rows_l), :],
                legendre_buf.at[pl.ds(row_l, rows_l), :],
                load_sems.at[1, index],
            ),
        )

    small = [
        pltpu.make_async_copy(source, target, small_sems.at[number])
        for number, (source, target) in enumerate(
            [
                (waves_hbm, waves_smem),
                (points_hbm, points_smem),
                (waves_hbm, waves_ref),
                (owners_hbm, owners_ref),
            ]
        )
    ]
    for copy in small:
        copy.start()
    for index in range(groups):
        for copy in loads(index):
            copy.start()
    lax.fori_loop(1, everyone, greet, 0)
    for copy in small:
        copy.wait()

    degree = lax.broadcasted_iota(I32, (pairs, degrees), 1)
    alternate = (1 - 2 * (degree % 2)).astype(F32).astype(BF16)
    lane = lax.broadcasted_iota(I32, (channels, rows_l), 1)
    out_lane = lax.broadcasted_iota(I32, (8, rows_l), 1)
    in_row = lax.broadcasted_iota(I32, (rows_l, rows_l), 0)

    def legendre_group(index):
        for copy in loads(index):
            copy.wait()
        row_s = pl.multiple_of(index * rows_s, rows_s)
        row_l = pl.multiple_of(index * rows_l, rows_l)
        north_rows = []
        south_rows = []
        for slot in range(group):
            limit = degrees - waves_smem[me * slots + index * group + slot]
            keep = jnp.where(degree < limit, 1.0, 0.0).astype(F32).astype(BF16)
            table = legendre_buf[pl.ds(pl.multiple_of(row_l + slot * pairs, pairs), pairs), :] * keep
            north_rows.append(table)
            south_rows.append(table * alternate)
        values = jnp.concatenate(
            [spectra_buf[0, pl.ds(row_s, rows_s), :], spectra_buf[1, pl.ds(row_s, rows_s), :]], 0
        )
        summed = []
        for part in range(2):
            rows = north_rows if part == 0 else south_rows
            products = nt_dot(values, jnp.concatenate(rows, 0)).reshape(2, group, channels, rows_l)
            picked = []
            for part_of in range(2):
                kept = jnp.zeros((channels, rows_l), F32)
                for slot in range(group):
                    kept = jnp.where(lane // pairs == slot, products[part_of, slot], kept)
                picked.append(kept)
            summed.append(picked)
        stacked = jnp.concatenate([summed[0][0], summed[1][0], summed[0][1], summed[1][1]], 0)
        dest_half = out_lane // LANES
        segment = (out_lane % LANES) // group
        dest = dest_half * segments + lax.rem(segment - index + segments, segments)
        origin = ((out_lane % group) * pairs + dest)[:1]
        permute = (in_row == origin).astype(F32).astype(BF16)
        permuted_buf[index] = jnp.dot(stacked.astype(BF16), permute, preferred_element_type=F32)

    for index in range(groups):
        legendre_group(index)

    lane_segment = lax.broadcasted_iota(I32, (4 * channels, LANES), 1) // group
    for pair in range(pairs):
        at = (pair // segments) * LANES
        gathered = jnp.zeros((4 * channels, LANES), F32)
        for index in range(groups):
            gathered = jnp.where(
                lane_segment == (pair % segments + index) % segments,
                permuted_buf[index, :, at : at + LANES],
                gathered,
            )
        first_send[(pair % per_fld) * fld + pair // per_fld] = gathered.astype(BF16)

    pl.semaphore_wait(barrier, everyone - 1)

    def first_copy(step):
        other = lax.rem(me + step, lat)
        return pltpu.make_async_remote_copy(
            src_ref=first_send.at[other],
            dst_ref=first_recv.at[me],
            send_sem=send_sems1.at[step],
            recv_sem=recv_sems1.at[step],
            device_id=(other, my_fld),
            device_id_type=MESH,
        )

    def first_start(step, carry):
        first_copy(step).start()
        return carry

    lax.fori_loop(1, lat, first_start, 0)

    points = jnp.full((1, LANES), points_smem[my_pair], I32).astype(F32)
    inverse = 1.0 / points

    def window_of(buffer, start):
        aligned = start // LANES * LANES
        chunk = buffer[:, pl.ds(pl.multiple_of(aligned, LANES), 2 * LANES)]
        chunk = jnp.broadcast_to(chunk, (8, 2 * LANES))
        return pltpu.roll(chunk, lax.rem(2 * LANES - (start - aligned), 2 * LANES), 1)[:, :LANES]

    table_rows = turn_cos.shape[1] + 2 * STEP
    row_index = lax.broadcasted_iota(I32, (table_rows, LANES), 0)
    index_column = jnp.where(
        row_index < STEP,
        row_index,
        jnp.where(row_index < 2 * STEP, (row_index - STEP) * STEP, (row_index - 2 * STEP) * WIDTH),
    ).astype(F32)

    wave_buf[...] = jnp.zeros(wave_buf.shape, I32)
    wave_buf[:, : lat * slots] = waves_ref[...].reshape(1, lat * slots)

    def make_tables(source, carry):
        wave_row = window_of(wave_buf, source * slots)
        wave_row = pltpu.roll(wave_row, lax.rem(my_pair, segments) * group, 1)[:1]
        cos_all, sin_all = turn_tables(wave_row.astype(F32), index_column, points, inverse)
        weight = jnp.where(wave_row == 0, 1.0, 2.0).astype(F32)
        turn_cos[source] = cos_all[2 * STEP :] * weight
        turn_sin[source] = sin_all[2 * STEP :] * weight
        cos_low, sin_low = cos_all[:STEP], sin_all[:STEP]
        for high in range(WIDTH // STEP):
            cos_high = cos_all[STEP + high : STEP + high + 1]
            sin_high = sin_all[STEP + high : STEP + high + 1]
            place = slice(high * STEP, (high + 1) * STEP)
            basis_buf[source, place, :LANES] = (cos_high * cos_low - sin_high * sin_low).astype(BF16)
            basis_buf[source, place, LANES:] = (sin_high * cos_low + cos_high * sin_low).astype(BF16)
        return carry

    lax.fori_loop(0, lat, make_tables, 0, unroll=4 if lat % 4 == 0 else 1)

    owner_buf[...] = jnp.zeros(owner_buf.shape, I32)
    owner_buf[:, : owners_ref.shape[1]] = owners_ref[...]
    owner_row = window_of(owner_buf, my_pair * 2 * BPR)[:1]
    owner_row = jnp.where(lax.broadcasted_iota(I32, (1, LANES), 1) < 2 * BPR, owner_row, -1)
    onehot = (lax.broadcasted_iota(I32, (lat, LANES), 0) == owner_row).astype(F32)
    upper = (
        lax.broadcasted_iota(I32, (LANES, LANES), 0) < lax.broadcasted_iota(I32, (LANES, LANES), 1)
    ).astype(F32)
    earlier = jnp.dot(onehot.astype(BF16), upper.astype(BF16), preferred_element_type=F32)
    rank_row = jnp.sum(onehot * earlier, axis=0, keepdims=True)
    which = lax.broadcasted_iota(I32, (16, LANES), 0)
    both = jnp.where(which == 0, owner_row.astype(F32), jnp.where(which == 1, rank_row, 0.0))
    total_columns = 2 * padded_rows
    column = lax.broadcasted_iota(I32, (8, total_columns), 1)
    half = column // padded_rows
    inner = column - half * padded_rows
    span = inner // (2 * channels)
    mirror = (inner // channels) % 2
    block = 2 * span + half
    valid = (inner < half_rows) & (block < BPR)
    number = jnp.where(valid, mirror * BPR + block, -1)[:1]
    expand = (lax.broadcasted_iota(I32, (LANES, total_columns), 0) == number).astype(F32)
    spread = jnp.dot(both.astype(BF16), expand.astype(BF16), preferred_element_type=F32)
    spread = spread.astype(I32)
    channel = column[:1] % channels
    target = spread[0:1] * slot_rows + spread[1:2] * channels + channel
    target = jnp.where(valid[:1], target, -1)

    def make_select(index, carry):
        start = pl.multiple_of(index * LANES, LANES)
        rows = lax.broadcasted_iota(I32, (LANES, total_columns), 0) + start
        select_buf[pl.ds(start, LANES), :] = (rows == target).astype(F32).astype(BF16)
        return carry

    lax.fori_loop(0, select_buf.shape[0] // LANES, make_select, 0)

    def accumulate(source, arrived, place_of):
        real = arrived[: 2 * channels].astype(F32)
        imag = arrived[2 * channels :].astype(F32)
        cos_rows = turn_cos[source]
        sin_rows = turn_sin[source]
        for span_index in range(blocks):
            cos_turn = cos_rows[span_index : span_index + 1]
            sin_turn = sin_rows[span_index : span_index + 1]
            place = slice(span_index * 2 * channels, (span_index + 1) * 2 * channels)
            rotated_buf[place_of, place, :LANES] = (real * cos_turn - imag * sin_turn).astype(BF16)
            rotated_buf[place_of, place, LANES:] = (-(real * sin_turn + imag * cos_turn)).astype(BF16)
        return nt_dot(rotated_buf[place_of], basis_buf[source])

    total_buf[...] = accumulate(me, first_send[me], 0)
    unrolled = rotated_buf.shape[0]

    def arrive(turn, carry):
        steps = [1 + turn * unrolled + within for within in range(unrolled)]
        for step in steps:
            first_copy(step).wait_recv()
        product = None
        for within, step in enumerate(steps):
            source = lax.rem(me + lat - step, lat)
            term = accumulate(source, first_recv[source], within)
            product = term if product is None else product + term
        total_buf[...] += product
        return carry

    lax.fori_loop(0, (lat - 1) // unrolled, arrive, 0)

    grid_buf[...] = jnp.zeros(grid_buf.shape, BF16)
    offset = lax.broadcasted_iota(I32, (2 * channels, WIDTH), 1)
    for span_index in range(blocks):
        low, high = span_index * 2 * channels, (span_index + 1) * 2 * channels
        inside = offset < points_smem[my_pair] - span_index * WIDTH
        grid = jnp.where(inside, total_buf[low:high], 0.0).astype(BF16)
        grid_buf[low:high, :] = grid[:, :CELL]
        grid_buf[padded_rows + low : padded_rows + high, :] = grid[:, CELL:]

    def second_copy(step):
        other = lax.rem(me + step, lat)
        return pltpu.make_async_remote_copy(
            src_ref=second_send.at[pl.ds(pl.multiple_of(other * slot_rows, slot_rows), slot_rows), :],
            dst_ref=out_ref.at[my_fld, mine],
            send_sem=send_sems2.at[step],
            recv_sem=recv_sems2.at[my_fld, mine],
            device_id=(other, home),
            device_id_type=MESH,
        )

    own_copy = pltpu.make_async_copy(
        second_send.at[pl.ds(pl.multiple_of(me * slot_rows, slot_rows), slot_rows), :],
        out_ref.at[my_fld, mine],
        local_sem,
    )

    together = 4 if lat % 4 == 0 else 1
    chunks = lat // together
    chunk_rows = together * slot_rows
    for turn in range(chunks):
        chunk = lax.rem(me // together + chunks // 2 + turn, chunks)
        rows = pl.ds(pl.multiple_of(chunk * chunk_rows, chunk_rows), chunk_rows)
        second_send[rows, :] = jnp.dot(
            select_buf[rows, :], grid_buf[...], preferred_element_type=F32
        ).astype(BF16)
        for within in range(together):
            step = lax.rem(chunk * together + within + lat - me, lat)
            stays = (step == 0) & (home == my_fld)

            @pl.when(stays)
            def _():
                own_copy.start()

            @pl.when(jnp.logical_not(stays))
            def _():
                second_copy(step).start()

    def first_done(step, carry):
        first_copy(step).wait_send()
        return carry

    lax.fori_loop(1, lat, first_done, 0)

    def second_done(step, carry):
        second_copy(step).wait_send()
        return carry

    lax.fori_loop(1, lat, second_done, 0)

    @pl.when(home == my_fld)
    def _():
        own_copy.wait()

    @pl.when(home != my_fld)
    def _():
        second_copy(0).wait_send()

    def from_source(step, carry):
        from_fld = step // per_fld
        from_pair = lax.rem(step, per_fld)
        is_self = (from_fld == my_fld) & (from_pair * fld + my_fld == me)

        @pl.when(jnp.logical_not(is_self))
        def _():
            pltpu.make_async_remote_copy(
                src_ref=second_send.at[pl.ds(0, slot_rows), :],
                dst_ref=out_ref.at[from_fld, from_pair],
                send_sem=send_sems2.at[0],
                recv_sem=recv_sems2.at[from_fld, from_pair],
                device_id=(me, my_fld),
                device_id_type=MESH,
            ).wait_recv()

        return carry

    lax.fori_loop(0, fld * per_fld, from_source, 0)


def on_device(lat, fld, spectra, legendre, wave_order, row_points, owners):
    slots, pairs, degrees = legendre.shape
    channels = spectra.shape[2]
    group = max(g for g in range(1, slots + 1) if slots % g == 0 and g * pairs <= 256 and LANES % g == 0)
    send_cap = max(2, (2 * BPR + lat - 1) // lat)
    blocks = -(-BPR * CELL // WIDTH)
    half_rows = blocks * 2 * channels
    padded_rows = -(-half_rows // LANES) * LANES
    turn_rows = -(-blocks // 8) * 8
    slot_rows = send_cap * channels
    select_rows = -(-lat * slot_rows // LANES) * LANES
    per_fld = pairs // fld
    dims = (lat, fld, pairs, slots, channels, degrees, group, send_cap, blocks)
    groups = slots // group
    unrolled = max(u for u in range(1, 6) if (lat - 1) % u == 0)
    anywhere = pl.BlockSpec(memory_space=pl.ANY)
    received = pl.pallas_call(
        functools.partial(fused_kernel, dims),
        out_shape=jax.ShapeDtypeStruct((fld, per_fld, slot_rows, CELL), BF16),
        in_specs=[anywhere] * 5,
        out_specs=anywhere,
        scratch_shapes=[
            pltpu.VMEM((2, slots * channels, degrees), BF16),
            pltpu.VMEM((slots * pairs, degrees), BF16),
            pltpu.VMEM((groups, 4 * channels, group * pairs), F32),
            pltpu.VMEM((pairs, 4 * channels, LANES), BF16),
            pltpu.VMEM((lat, 4 * channels, LANES), BF16),
            pltpu.VMEM((lat, WIDTH, 2 * LANES), BF16),
            pltpu.VMEM((lat, turn_rows, LANES), F32),
            pltpu.VMEM((lat, turn_rows, LANES), F32),
            pltpu.VMEM((unrolled, half_rows, 2 * LANES), BF16),
            pltpu.VMEM((half_rows, WIDTH), F32),
            pltpu.VMEM((2 * padded_rows, CELL), BF16),
            pltpu.VMEM((select_rows, 2 * padded_rows), BF16),
            pltpu.VMEM((lat * slot_rows, CELL), BF16),
            pltpu.SemaphoreType.DMA((2, groups)),
            pltpu.SemaphoreType.DMA((lat,)),
            pltpu.SemaphoreType.DMA((lat,)),
            pltpu.SemaphoreType.DMA((lat,)),
            pltpu.SemaphoreType.DMA((fld, per_fld)),
            pltpu.SemaphoreType.DMA,
            pltpu.VMEM((1, -(-wave_order.shape[0] // LANES) * LANES + 2 * LANES), I32),
            pltpu.VMEM((1, -(-owners.shape[0] // LANES) * LANES + 2 * LANES), I32),
            pltpu.SMEM(wave_order.shape, I32),
            pltpu.SMEM(row_points.shape, I32),
            pltpu.VMEM(wave_order.shape, I32),
            pltpu.VMEM((1, owners.shape[0]), I32),
            pltpu.SemaphoreType.DMA((4,)),
        ],
        compiler_params=pltpu.CompilerParams(
            collective_id=0, has_side_effects=True, vmem_limit_bytes=60000 * 1024
        ),
    )(
        wave_order,
        row_points,
        spectra.reshape(2, slots * channels, degrees),
        legendre.reshape(slots * pairs, degrees),
        owners.reshape(1, pairs * 2 * BPR),
    )
    split = received.reshape(fld, per_fld * send_cap, channels, CELL)
    return jnp.transpose(split, (1, 0, 2, 3)).reshape(per_fld * send_cap, fld * channels, CELL)


def solution(mesh):
    return jax.shard_map(
        functools.partial(on_device, mesh.shape["lat"], mesh.shape["fld"]),
        mesh=mesh,
        in_specs=(P(None, "lat", "fld", None), P("lat", None, None), P(), P(), P()),
        out_specs=P(("lat", "fld"), None, None),
        check_vma=False,
    )
```
